512 devices in a mesh: grp: 16 (over z), sub: 32 (over x, y, core).
Axes of the slice: x: 4, y: 4, z: 16, core: 2. Of those that a mesh axis runs over, the one named last changes fastest.
Arguments:
- leaf_bases: bfloat16 [6144, 256, 128], P(('grp', 'sub')), may hold values from -6 to 6
- leaf_transfers: bfloat16 [6144, 128, 128], P(('grp', 'sub')), may hold values from -1 to 2
- leaf_blocks: bfloat16 [6144, 6, 128, 128], P(('grp', 'sub')), may hold values from -6 to 6
- leaf_partner_dev: int32 [6144, 6], P(('grp', 'sub')), may hold values from 0 to 31, all different within a row; in each aligned block of 12 rows (0 to 11, 12 to 23, ...) at most 5 rows name the same one
- leaf_partner_slot: int32 [6144, 6], P(('grp', 'sub')), may hold values from 0 to 11
- parent_blocks: bfloat16 [3072, 3, 128, 128], P(('grp', 'sub')), may hold values from -6 to 6
- parent_partner_group: int32 [3072, 3], P(('grp', 'sub')), may hold values from 0 to 15, all different within a row; in each aligned block of 6 rows (0 to 5, 6 to 11, ...) at most 3 rows name the same one
- parent_partner_slot: int32 [3072, 3], P(('grp', 'sub')), may hold values from 0 to 5
- leaf_start: float32 [64, 128], replicated, may hold values from -6 to 6
- parent_start: float32 [64, 128], replicated, may hold values from -6 to 6
Outputs:
- new_leaf_bases: bfloat16 [6144, 64, 256], P(('grp', 'sub'))
- new_leaf_blocks: bfloat16 [6144, 6, 4096], P(('grp', 'sub'))
- new_parent_blocks: bfloat16 [3072, 3, 4096], P(('grp', 'sub'))
The draws below stay inside these ranges and needn't reach their ends.
Inputs may be any that keep to these rules, and one draw needn't show every extreme that they name: `leaf_partner_dev`: one leaf's partners lie on different devices of its group; among the leaves of one device no index appears more than 5 times, and that count is reached on some device. `parent_partner_group`: one parent's partners lie in different groups; among the parents of one device no group appears more than 3 times, and that count is reached on some device.
All inputs are finite; a program needn't handle non-finite values.
Results may differ from the reference program's by a relative error of at most 0.033.
Values may be sent and summed in bfloat16 or wider, within the bound.
A program may use at most 64 MiB of HBM per device.

```python
import math
import jax
import jax.numpy as jnp
import numpy as np
from jax import lax

K = 128
R = 64
LEAF_DEV = 12
LEAF_ROWS = 256
NC_IN = 6
NC_X = 3
PAR_DEV = 6
NLEAF = 6144
NPAR = 3072
CAP_IN = 5
CAP_X = 3
N_GRP = 16
N_SUB = 32


def draw_leaf_transfers(key, part):
    noise = jnp.clip(jax.random.normal(key, (NLEAF, K, K), jnp.float32), -4.0, 4.0)
    identity = jnp.eye(K, dtype=jnp.float32)[None, :, :]
    return (identity + 0.5 * noise / math.sqrt(K)).astype(jnp.bfloat16)


def place_ends(values, own_key, least, largest):
    extent = values.shape
    spot = [jax.random.randint(jax.random.fold_in(own_key, axis), (), 0, extent[axis]) for axis in range(len(extent))]
    values = values.at[tuple(spot)].set(least)
    longest = extent.index(max(extent))
    spot[longest] = (spot[longest] + 1) % extent[longest]
    return values.at[tuple(spot)].set(largest)


def level_of(stream_key, shape, cuts, low, largest):
    gain, own = 1.0, jax.random.fold_in(stream_key, 6)
    for axis_at, shards_of in cuts:
        heights = jnp.exp(jax.random.uniform(jax.random.fold_in(own, axis_at), (shards_of,), jnp.float32, low / len(cuts), largest / len(cuts)))
        gain = gain * jnp.repeat(heights, shape[axis_at] // shards_of).reshape([-1 if axis == axis_at else 1 for axis in range(len(shape))])
    return gain


def routed_block(own_key, own, number, rows, number_of, top, bound, lean):
    order = jax.random.permutation(own_key, number_of)
    packed, ordinary = shares(number_of, rows * top, bound, lean, True), shares(number_of, rows * top, bound, lean, False)
    places = jnp.arange(number_of)

    def named(lengths, turn):
        used = int((lengths > 0).sum())
        fixed = max(1, used // 4)
        shifted = fixed + (places - fixed + turn * (used - fixed)) % max(1, number_of - fixed)
        return jnp.zeros((number_of,), jnp.int32).at[order[jnp.where(places < fixed, places, shifted)]].set(jnp.asarray(lengths, jnp.int32))

    lengths = jnp.where(number % 4 == 0, named(packed, number // 4), named(ordinary, number - number // 4 - 1))
    mixed = jax.random.permutation(jax.random.fold_in(own, 3), number_of)
    donor, taker = mixed[0:number_of // 2 * 2:2], mixed[1:number_of // 2 * 2:2]
    slack = jnp.minimum(lengths[donor] - 1, bound - lengths[taker]) // 2
    slack = jnp.where((donor == order[0]) | (taker == order[0]) | (lengths[taker] == 0), 0, jnp.maximum(slack, 0))
    shifted = jax.random.randint(jax.random.fold_in(own, 4), (number_of // 2,), 0, 1 << 20) % (slack + 1)
    lengths = lengths.at[donor].add(-shifted).at[taker].add(shifted)
    items = jnp.searchsorted(jnp.cumsum(lengths), jnp.arange(rows * top), side="right").astype(jnp.int32)
    grid = items.reshape(top, rows).T
    grid = grid[jax.random.permutation(jax.random.fold_in(own, 1), rows)]
    turn = jax.random.randint(jax.random.fold_in(own, 2), (rows, 1), 0, top)
    return jnp.take_along_axis(grid, (jnp.arange(top)[None, :] + turn) % top, axis=1)


def shares(amount, total, bound, skew, full):
    loads = [(1 << 20) // math.isqrt(standing ** skew) + 1 for standing in range(1, amount + 1)]
    largest = bound if full else min(bound, max(-(-total // amount), total * loads[0] // sum(loads)))
    least = 1 if total - largest >= amount - 1 else 0
    counts, surplus = [largest] + [least] * (amount - 1), total - largest - least * (amount - 1)
    while surplus > 0:
        candidates = [i for i in range(1, amount) if counts[i] < largest] or [i for i in range(1, amount) if counts[i] < bound]
        mass, budget = sum([loads[i] for i in candidates]), surplus
        for i in candidates:
            addition = min(bound - counts[i], max(1, budget * loads[i] // mass), surplus)
            counts[i] = counts[i] + addition
            surplus = surplus - addition
    return np.array(counts)


def bell_draw(stream_key, extent, spread, most, cuts=(), held_as=jnp.bfloat16):
    result = jax.random.normal(stream_key, extent, jnp.float32) * spread
    if len(cuts) > 0:
        result = level_of(stream_key, extent, cuts, -0.22, 0.18) * result
    return jnp.clip(result, min=-most, max=most).astype(held_as)


def setup_inputs(seed: int = 0) -> dict:
    splits = jax.random.split(jax.random.key(seed), 11)
    leaf_bases = bell_draw(splits[0], (NLEAF, LEAF_ROWS, K), 1.0, 6.0, ((0, 512),))
    leaf_transfers = draw_leaf_transfers(jax.random.fold_in(splits[10], 71), 0)
    leaf_blocks = bell_draw(splits[2], (NLEAF, NC_IN, K, K), 1.0, 6.0, ((0, 512),))
    leaf_partner_dev_keys = jax.random.split(jax.random.fold_in(splits[3], 1), NLEAF // LEAF_DEV)
    leaf_partner_dev_turns = jax.random.permutation(jax.random.fold_in(splits[3], 3), NLEAF // LEAF_DEV)
    leaf_partner_dev = jax.vmap(lambda own, number: routed_block(jax.random.fold_in(splits[3], 2), own, number, LEAF_DEV, N_SUB, NC_IN, CAP_IN, 2))(leaf_partner_dev_keys, leaf_partner_dev_turns).reshape((NLEAF, NC_IN))
    leaf_partner_slot = place_ends(jax.random.randint(splits[4], (NLEAF, NC_IN), 0, LEAF_DEV), jax.random.fold_in(splits[4], 1), 0, LEAF_DEV - 1).astype(jnp.int32)
    parent_blocks = bell_draw(splits[5], (NPAR, NC_X, K, K), 1.0, 6.0, ((0, 512),))
    parent_partner_group_keys = jax.random.split(jax.random.fold_in(splits[6], 1), NPAR // PAR_DEV)
    parent_partner_group_turns = jax.random.permutation(jax.random.fold_in(splits[6], 3), NPAR // PAR_DEV)
    parent_partner_group = jax.vmap(lambda own, number: routed_block(jax.random.fold_in(splits[6], 2), own, number, PAR_DEV, N_GRP, NC_X, CAP_X, 2))(parent_partner_group_keys, parent_partner_group_turns).reshape((NPAR, NC_X))
    parent_partner_slot = place_ends(jax.random.randint(splits[7], (NPAR, NC_X), 0, PAR_DEV), jax.random.fold_in(splits[7], 1), 0, PAR_DEV - 1).astype(jnp.int32)
    leaf_start = bell_draw(splits[8], (R, K), 1.0, 6.0, (), jnp.float32)
    parent_start = bell_draw(splits[9], (R, 2 * R), 1.0, 6.0, (), jnp.float32)
    return {"leaf_bases": leaf_bases, "leaf_transfers": leaf_transfers, "leaf_blocks": leaf_blocks, "leaf_partner_dev": leaf_partner_dev, "leaf_partner_slot": leaf_partner_slot, "parent_blocks": parent_blocks, "parent_partner_group": parent_partner_group, "parent_partner_slot": parent_partner_slot, "leaf_start": leaf_start, "parent_start": parent_start}


TOP_PRECISION = lax.Precision.HIGHEST

def single(values):
    return values.astype(jnp.float32)

def subspace(weight, start_rows):
    basis_rows = jnp.broadcast_to(start_rows, (weight.shape[0],) + start_rows.shape)
    image_rows = jnp.einsum('brn,bnm->brm', basis_rows, weight, precision=TOP_PRECISION)
    image_rows = jnp.einsum('brn,bnm->brm', image_rows, weight, precision=TOP_PRECISION)
    cross_gram = jnp.einsum('brn,bsn->brs', image_rows, image_rows, precision=TOP_PRECISION)
    factor = jnp.linalg.cholesky(cross_gram)
    return jax.scipy.linalg.solve_triangular(factor, image_rows, lower=True)

def reference(leaf_bases, leaf_transfers, leaf_blocks, leaf_partner_dev, leaf_partner_slot, parent_blocks, parent_partner_group, parent_partner_slot, leaf_start, parent_start):
    devices_all = N_GRP * N_SUB
    device_ids = jnp.arange(devices_all, dtype=jnp.int32)
    leaf_slots = jnp.arange(LEAF_DEV, dtype=jnp.int32)
    parent_slots = jnp.arange(PAR_DEV, dtype=jnp.int32)

    def parent_section_one(device):
        blocks = single(lax.dynamic_slice_in_dim(parent_blocks, device * PAR_DEV, PAR_DEV, 0))
        return jnp.einsum('pckl,pcml->pkm', blocks, blocks, precision=TOP_PRECISION)
    parent_weight = lax.map(parent_section_one, device_ids).reshape(NPAR, K, K)

    def leaf_section(device):
        pair_offset = device // 2 * 2
        owners = (pair_offset + leaf_slots // PAR_DEV) * PAR_DEV + leaf_slots % PAR_DEV
        descended = parent_weight[owners]
        transfers = single(lax.dynamic_slice_in_dim(leaf_transfers, device * LEAF_DEV, LEAF_DEV, 0))
        blocks = single(lax.dynamic_slice_in_dim(leaf_blocks, device * LEAF_DEV, LEAF_DEV, 0))
        weight = jnp.einsum('jckl,jcml->jkm', blocks, blocks, precision=TOP_PRECISION)
        carried = jnp.einsum('jka,jab->jkb', transfers, descended, precision=TOP_PRECISION)
        weight = weight + jnp.einsum('jkb,jmb->jkm', carried, transfers, precision=TOP_PRECISION)
        change = lax.optimization_barrier(subspace(weight, leaf_start).astype(jnp.bfloat16))
        projected = jnp.einsum('jrk,jkm->jrm', single(change), transfers, precision=TOP_PRECISION)
        bases = single(lax.dynamic_slice_in_dim(leaf_bases, device * LEAF_DEV, LEAF_DEV, 0))
        new_bases = jnp.einsum('jrk,jnk->jrn', single(change), bases, precision=TOP_PRECISION).astype(jnp.bfloat16)
        return (change, projected, new_bases)
    change_all, projected_all, new_leaf_bases = lax.map(leaf_section, device_ids)
    change_all = change_all.reshape(NLEAF, R, K)
    projected_all = projected_all.reshape(NLEAF, R, K)
    new_leaf_bases = new_leaf_bases.reshape(NLEAF, R, LEAF_ROWS)

    def parent_section_two(device):
        pair_offset = device // 2 * 2
        column = device % 2 * PAR_DEV + parent_slots
        first_child = projected_all[pair_offset * LEAF_DEV + column]
        second_child = projected_all[(pair_offset + 1) * LEAF_DEV + column]
        stacked = jnp.concatenate([first_child, second_child], axis=1)
        weight = lax.dynamic_slice_in_dim(parent_weight, device * PAR_DEV, PAR_DEV, 0)
        parent_left = jnp.einsum('prk,pkm->prm', stacked, weight, precision=TOP_PRECISION)
        parent_gram = jnp.einsum('prm,psm->prs', parent_left, stacked, precision=TOP_PRECISION)
        parent_rows = subspace(parent_gram, parent_start)
        return jnp.einsum('prs,psk->prk', parent_rows, stacked, precision=TOP_PRECISION).astype(jnp.bfloat16)
    parent_change = lax.optimization_barrier(lax.map(parent_section_two, device_ids).reshape(NPAR, R, K))

    def couple_leaves(device):
        group_base = device // N_SUB * N_SUB
        dev_rows = lax.dynamic_slice_in_dim(leaf_partner_dev, device * LEAF_DEV, LEAF_DEV, 0)
        slot_rows = lax.dynamic_slice_in_dim(leaf_partner_slot, device * LEAF_DEV, LEAF_DEV, 0)
        partner = (group_base + dev_rows) * LEAF_DEV + slot_rows
        distant_site = single(change_all[partner])
        own_rows = single(lax.dynamic_slice_in_dim(change_all, device * LEAF_DEV, LEAF_DEV, 0))
        blocks = single(lax.dynamic_slice_in_dim(leaf_blocks, device * LEAF_DEV, LEAF_DEV, 0))
        leaf_midpoint = jnp.einsum('jrk,jckl->jcrl', own_rows, blocks, precision=TOP_PRECISION).astype(jnp.bfloat16)
        leaf_midpoint = single(lax.optimization_barrier(leaf_midpoint))
        final_output = jnp.einsum('jcrl,jcsl->jcrs', leaf_midpoint, distant_site, precision=TOP_PRECISION).astype(jnp.bfloat16)
        return final_output.reshape(LEAF_DEV, NC_IN, R * R)
    new_leaf_blocks = lax.map(couple_leaves, device_ids).reshape(NLEAF, NC_IN, R * R)

    def couple_parents(device):
        inner_index = device % N_SUB
        group_rows = lax.dynamic_slice_in_dim(parent_partner_group, device * PAR_DEV, PAR_DEV, 0)
        slot_rows = lax.dynamic_slice_in_dim(parent_partner_slot, device * PAR_DEV, PAR_DEV, 0)
        partner = (group_rows * N_SUB + inner_index) * PAR_DEV + slot_rows
        distant_site = single(parent_change[partner])
        own_rows = single(lax.dynamic_slice_in_dim(parent_change, device * PAR_DEV, PAR_DEV, 0))
        blocks = single(lax.dynamic_slice_in_dim(parent_blocks, device * PAR_DEV, PAR_DEV, 0))
        parent_midpoint = jnp.einsum('prk,pckl->pcrl', own_rows, blocks, precision=TOP_PRECISION).astype(jnp.bfloat16)
        parent_midpoint = single(lax.optimization_barrier(parent_midpoint))
        final_output = jnp.einsum('juog,juqg->juoq', parent_midpoint, distant_site, precision=TOP_PRECISION).astype(jnp.bfloat16)
        return final_output.reshape(PAR_DEV, NC_X, R * R)
    new_parent_blocks = lax.map(couple_parents, device_ids).reshape(NPAR, NC_X, R * R)
    return (new_leaf_bases, new_leaf_blocks, new_parent_blocks)
```

```python
import functools

import jax
import jax.numpy as jnp
from jax import lax
from jax.experimental import pallas as pl
from jax.experimental.pallas import tpu as pltpu
from jax.sharding import PartitionSpec as P

HIGHEST = lax.Precision.HIGHEST
MESH = pl.DeviceIdType.MESH
F32 = jnp.float32
BF16 = jnp.bfloat16
SIDE = 4


def nt(left, right, precision=None):
    return lax.dot_general(
        left, right, (((1,), (1,)), ((), ())), precision=precision, preferred_element_type=F32
    )


def nn(left, right, precision=None):
    return lax.dot_general(
        left, right, (((1,), (0,)), ((), ())), precision=precision, preferred_element_type=F32
    )


def partner(block, axis, apart):
    count = lax.axis_size(axis)
    route = []
    for low in range(count):
        high = low | 1 << apart
        if high != low and high < count:
            route += [(low, high), (high, low)]
    return lax.ppermute(block, axis, route)


def eliminate(joined):
    count, rows, width = joined.shape
    lane = rows
    tiles = [joined[:, 8 * i : 8 * i + 8, :] for i in range(rows // 8)]
    full = (count, 8, width)
    place = lax.broadcasted_iota(jnp.int32, full, 1)
    for at in range(rows // 8):
        scale = jnp.zeros(full, F32)
        for inner in range(8):
            k = lane + at * 8 + inner
            tile = tiles[at]
            column = jnp.broadcast_to(tile[:, :, k : k + 1], full)
            pivot = jnp.broadcast_to(column[:, inner : inner + 1, :], full)
            row = jnp.broadcast_to(tile[:, inner : inner + 1, :], full) * (1.0 / pivot)
            scale = jnp.where(place == inner, lax.rsqrt(pivot), scale)
            tiles[at] = tile - jnp.where(place > inner, column, 0.0) * row
            for i in range(at + 1, rows // 8):
                tiles[i] = tiles[i] - jnp.broadcast_to(tiles[i][:, :, k : k + 1], full) * row
        tiles[at] = tiles[at] * scale
    return jnp.concatenate(tiles, axis=1)


def begin_subspace(start, weight):
    rows, width = start.shape
    image = nn(nn(start, weight, HIGHEST), weight, HIGHEST)
    first = lax.broadcasted_iota(jnp.int32, (rows, width), 0)
    second = lax.broadcasted_iota(jnp.int32, (rows, width), 1)
    unit = jnp.where(first == second, 1.0, 0.0)
    gram = nt(image, jnp.concatenate([jnp.zeros_like(image), image], axis=0), HIGHEST)
    return image, gram + unit


def end_subspace(joined, image):
    return nn(joined, jnp.concatenate([image, jnp.zeros_like(image)], axis=0), HIGHEST)


def parent_weight_kernel(blocks_ref, weight_ref, sent_ref):
    count, links = blocks_ref.shape[:2]

    @pl.loop(0, count)
    def _(p):
        total = nt(blocks_ref[p, 0], blocks_ref[p, 0])
        for c in range(1, links):
            total = total + nt(blocks_ref[p, c], blocks_ref[p, c])
        weight_ref[p] = total
        sent_ref[p] = total.astype(BF16)


def leaf_weight_kernel(blocks_ref, weight_ref):
    count, links = blocks_ref.shape[:2]

    @pl.loop(0, count)
    def _(t):
        total = None
        for c in range(0, links, 2):
            pair = jnp.concatenate([blocks_ref[t, c], blocks_ref[t, c + 1]], axis=1)
            product = nt(pair, pair)
            total = product if total is None else total + product
        weight_ref[t] = total


def leaf_kernel(
    weight_ref, own_ref, other_ref, transfers_ref, start_ref,
    change_ref, kept_ref, sent_ref, joined_ref, image_ref,
):
    count = weight_ref.shape[0]
    half = own_ref.shape[0]
    member = lax.rem(lax.axis_index("sub"), 2)

    def prepare(t, descended):
        transfer = transfers_ref[t].astype(F32)
        carried = nn(transfer, descended, HIGHEST)
        weight = weight_ref[t] + nt(carried, transfer, HIGHEST)
        image_ref[t], joined_ref[t] = begin_subspace(start_ref[...], weight)

    @pl.loop(0, half)
    def _(p):
        prepare(member * half + p, own_ref[p])
        prepare((1 - member) * half + p, other_ref[p].astype(F32))

    joined_ref[...] = eliminate(joined_ref[...])

    def finish(t):
        change = end_subspace(joined_ref[t], image_ref[t]).astype(BF16)
        change_ref[t] = change
        return nn(change, transfers_ref[t])

    @pl.loop(0, half)
    def _(p):
        kept_ref[p] = finish(member * half + p)
        sent_ref[p] = finish((1 - member) * half + p).astype(BF16)


def parent_kernel(weight_ref, kept_ref, received_ref, start_ref, change_ref, joined_ref, image_ref, stacked_ref):
    count = weight_ref.shape[0]
    first = lax.rem(lax.axis_index("sub"), 2) == 0

    @pl.loop(0, count)
    def _(p):
        kept, received = kept_ref[p], received_ref[p].astype(F32)
        stacked = jnp.concatenate(
            [jnp.where(first, kept, received), jnp.where(first, received, kept)], axis=0
        )
        stacked_ref[p] = stacked
        gram = nt(nn(stacked, weight_ref[p], HIGHEST), stacked, HIGHEST)
        image_ref[p], joined_ref[p] = begin_subspace(start_ref[...], gram)

    joined_ref[...] = eliminate(joined_ref[...])

    @pl.loop(0, count)
    def _(p):
        rows = end_subspace(joined_ref[p], image_ref[p])
        change_ref[p] = nn(rows, stacked_ref[p], HIGHEST).astype(BF16)


def couple_kernel(
    groups,
    leaf_dev_ref, leaf_slot_ref, parent_group_ref, parent_slot_ref,
    change_ref, parent_change_ref, bases_ref, leaf_blocks_ref, parent_blocks_ref,
    bases_out, leaf_out, parent_out,
    leaves, parents, half_rows, parent_half_rows, staged,
    local_sem, leaf_send, leaf_recv, ring_send, ring_recv,
):
    count, links = leaf_blocks_ref.shape[:2]
    parent_count, parent_links = parent_blocks_ref.shape[:2]
    rank = change_ref.shape[1]
    part = count // 2
    chunk = parent_count // 2
    sub, grp = lax.axis_index("sub"), lax.axis_index("grp")
    across, along, core = sub // (2 * SIDE), (sub // 2) % SIDE, sub % 2

    def site(x, y, c):
        return ((x + SIDE) % SIDE * SIDE + (y + SIDE) % SIDE) * 2 + c

    def near(h, outer, inner):
        if h == 0:
            return site(across + inner, along + outer, core)
        return site(across + outer, along + inner, core)

    outer_at = (along, across)
    inner_at = (across, along)

    def row_start(h, outer):
        return ((h * 2 + core) * SIDE + (outer + SIDE) % SIDE) * SIDE * part

    def block_start(h, outer, inner):
        return row_start(h, outer) + (inner + SIDE) % SIDE * part

    up, down = (grp + 1) % groups, (grp + groups - 1) % groups
    sibling = site(across, along, 1 - core)

    barrier = pltpu.get_barrier_semaphore()
    for target in (near(0, 0, 1), near(0, 0, -1), near(0, 1, 0), near(0, -1, 0), sibling):
        pl.semaphore_signal(barrier, inc=1, device_id={"sub": target}, device_id_type=MESH)
    for target in (up, down):
        pl.semaphore_signal(barrier, inc=1, device_id={"grp": target}, device_id_type=MESH)

    started = []

    def send_leaf(number, src, start, size, target):
        copy = pltpu.make_async_remote_copy(
            src_ref=src,
            dst_ref=leaves.at[pl.ds(start, size)],
            send_sem=leaf_send.at[number],
            recv_sem=leaf_recv.at[number],
            device_id={"sub": target},
            device_id_type=MESH,
        )
        copy.start()
        started.append(copy)
        return copy

    def pass_leaf(number, start, size, target):
        return send_leaf(number, leaves.at[pl.ds(start, size)], start, size, target)

    def send_parent(way, step, piece):
        number = (way * 8 + step) * 2 + piece
        origin = (grp - step + groups) % groups if way == 0 else (grp + step) % groups
        at = origin * parent_count + piece * chunk
        src = parent_change_ref.at[pl.ds(piece * chunk, chunk)] if step == 0 else parents.at[pl.ds(at, chunk)]
        copy = pltpu.make_async_remote_copy(
            src_ref=src,
            dst_ref=parents.at[pl.ds(at, chunk)],
            send_sem=ring_send.at[number],
            recv_sem=ring_recv.at[number],
            device_id={"grp": up if way == 0 else down},
            device_id_type=MESH,
        )
        copy.start()
        started.append(copy)
        return copy

    local = [
        pltpu.make_async_copy(
            change_ref.at[pl.ds(h * part, part)],
            leaves.at[pl.ds(block_start(h, outer_at[h], inner_at[h]), part)],
            local_sem.at[h],
        )
        for h in range(2)
    ]
    local.append(
        pltpu.make_async_copy(
            parent_change_ref, parents.at[pl.ds(grp * parent_count, parent_count)], local_sem.at[2]
        )
    )
    for copy in local:
        copy.start()

    pl.semaphore_wait(barrier, 7)

    inner_up, inner_down = [], []
    for h in range(2):
        own = change_ref.at[pl.ds(h * part, part)]
        start = block_start(h, outer_at[h], inner_at[h])
        inner_up.append(send_leaf(h * 2, own, start, part, near(h, 0, 1)))
        inner_down.append(send_leaf(h * 2 + 1, own, start, part, near(h, 0, -1)))
    ring = {}
    for piece in range(2):
        for way in range(2):
            ring[way, 0, piece] = send_parent(way, 0, piece)

    def ring_step(step):
        for piece in range(2):
            for way in range(2):
                if (way, step, piece) not in ring:
                    continue
                ring[way, step, piece].wait_recv()
                if step < groups // 2 - 2 or (step == groups // 2 - 2 and way == piece):
                    ring[way, step + 1, piece] = send_parent(way, step + 1, piece)

    row = lax.broadcasted_iota(jnp.int32, (rank, rank), 0)
    column = lax.broadcasted_iota(jnp.int32, (rank, rank), 1)
    low = rank // 2
    order = jnp.where(row < low, 2 * row, 2 * (row - low) + 1)
    shuffle = jnp.where(column == order, 1.0, 0.0).astype(BF16)

    @pl.loop(0, count)
    def _(t):
        bases_out[t] = nt(change_ref[t], bases_ref[t]).astype(BF16)

    for h in range(2):
        inner_up[h].wait_recv()
        inner_down[h].wait_recv()
    second_up, second_down = [], []
    cut = part // 2
    for h in range(2):
        outer, inner = outer_at[h], inner_at[h]
        second_up.append(
            pass_leaf(4 + h * 2, block_start(h, outer, inner - 1), cut, near(h, 0, 1))
        )
        second_down.append(
            pass_leaf(5 + h * 2, block_start(h, outer, inner + 1) + cut, part - cut, near(h, 0, -1))
        )
    ring_step(0)

    @pl.loop(0, parent_count)
    def _(p):
        mixed = nn(shuffle, parent_change_ref[p]).astype(BF16)
        for c in range(parent_links):
            parent_half_rows[p * parent_links + c] = nn(mixed, parent_blocks_ref[p, c]).astype(BF16)

    for h in range(2):
        second_up[h].wait_recv()
        second_down[h].wait_recv()
    for copy in local:
        copy.wait()
    size = SIDE * part
    cut = size // 2
    rows_up, rows_down, rest_up, rest_down = [], [], [], []
    for h in range(2):
        start = row_start(h, outer_at[h])
        rows_up.append(pass_leaf(8 + h * 6, start, cut, near(h, 1, 0)))
        rows_down.append(pass_leaf(9 + h * 6, start + cut, size - cut, near(h, -1, 0)))
    for h in range(2):
        start = row_start(h, outer_at[h])
        rest_up.append(pass_leaf(10 + h * 6, start + cut, size - cut, near(h, 1, 0)))
        rest_down.append(pass_leaf(11 + h * 6, start, cut, near(h, -1, 0)))
    shared = [pass_leaf(20 + h * 4, row_start(h, outer_at[h]), size, sibling) for h in range(2)]
    ring_step(1)

    @pl.loop(0, count)
    def _(t):
        mixed = nn(shuffle, change_ref[t]).astype(BF16)
        for c in range(links):
            half_rows[t * links + c] = nn(mixed, leaf_blocks_ref[t, c]).astype(BF16)

    ring_step(2)
    ring_step(3)
    ring_step(4)
    last_up, last_down = [], []
    for h in range(2):
        rows_up[h].wait_recv()
        last_up.append(pass_leaf(12 + h * 6, row_start(h, outer_at[h] - 1), cut, near(h, 1, 0)))
        rows_down[h].wait_recv()
        last_down.append(
            pass_leaf(13 + h * 6, row_start(h, outer_at[h] + 1) + cut, size - cut, near(h, -1, 0))
        )
    ring_step(5)
    ring_step(6)
    for h in range(2):
        rest_up[h].wait_recv()
        shared.append(pass_leaf(21 + h * 4, row_start(h, outer_at[h] - 1), size, sibling))
        rest_down[h].wait_recv()
        shared.append(pass_leaf(22 + h * 4, row_start(h, outer_at[h] + 1), size, sibling))
    ring_step(7)

    blank = jnp.zeros((rank, 2 * rank), BF16)

    def couple(half_pair, distant):
        pair = jnp.concatenate([half_pair[:low], half_pair[low:]], axis=1)
        twice = jnp.concatenate(
            [
                jnp.concatenate([distant, blank], axis=1),
                jnp.concatenate([blank, distant], axis=1),
            ],
            axis=0,
        )
        return nt(pair, twice)

    def flatten(out, at, width):
        for q in range(low):
            rows = staged[pl.ds(q, width, stride=low), :]
            out[at, :, 2 * rank * q : 2 * rank * (q + 1)] = rows.astype(BF16)

    @pl.loop(0, parent_count)
    def _(p):
        for c in range(parent_links):
            index = parent_group_ref[p, c] * parent_count + parent_slot_ref[p, c]
            staged[low * c : low * (c + 1), :] = couple(
                parent_half_rows[p * parent_links + c], parents[index]
            )
        flatten(parent_out, p, parent_links)

    for h in range(2):
        last_up[h].wait_recv()
        last_down[h].wait_recv()
        shared.append(pass_leaf(23 + h * 4, row_start(h, outer_at[h] + 2), size, sibling))
    for copy in shared:
        copy.wait_recv()

    @pl.loop(0, count)
    def _(t):
        for c in range(links):
            place, slot = leaf_dev_ref[t, c], leaf_slot_ref[t, c]
            x, y, z = place // (2 * SIDE), place // 2 % SIDE, place % 2
            h = slot // part
            outer, inner = y + h * (x - y), x + h * (y - x)
            index = (((h * 2 + z) * SIDE + outer) * SIDE + inner) * part + slot - h * part
            staged[low * c : low * (c + 1), :] = couple(half_rows[t * links + c], leaves[index])
        flatten(leaf_out, t, links)

    for copy in started:
        copy.wait_send()


def shards(
    leaf_bases,
    leaf_transfers,
    leaf_blocks,
    leaf_partner_dev,
    leaf_partner_slot,
    parent_blocks,
    parent_partner_group,
    parent_partner_slot,
    leaf_start,
    parent_start,
):
    leaf_count, leaf_links = leaf_blocks.shape[:2]
    half_count, parent_links = parent_blocks.shape[:2]
    rank_new, rank_old = leaf_start.shape
    points = leaf_bases.shape[1]
    groups, members = lax.axis_size("grp"), lax.axis_size("sub")
    square = (rank_old, rank_old)
    block = (rank_new, rank_old)

    def shape(*sizes, dtype=F32):
        return jax.ShapeDtypeStruct(sizes, dtype)

    parent_weight, parent_sent = pl.pallas_call(
        parent_weight_kernel,
        out_shape=(shape(half_count, *square), shape(half_count, *square, dtype=BF16)),
        name="parent_weight",
    )(parent_blocks)
    other_weight = partner(parent_sent, "sub", 0)
    leaf_weight = pl.pallas_call(
        leaf_weight_kernel,
        out_shape=shape(leaf_count, *square),
        cost_estimate=pl.CostEstimate(
            flops=2 * leaf_count * leaf_links * rank_old**3, bytes_accessed=3 << 20, transcendentals=0
        ),
        name="leaf_weight",
    )(leaf_blocks)
    change, kept, sent = pl.pallas_call(
        leaf_kernel,
        out_shape=(
            shape(leaf_count, *block, dtype=BF16),
            shape(half_count, *block),
            shape(half_count, *block, dtype=BF16),
        ),
        scratch_shapes=[pltpu.VMEM((leaf_count, *block), F32)] * 2,
        name="leaf_rows",
    )(leaf_weight, parent_weight, other_weight, leaf_transfers, leaf_start)
    received = partner(sent, "sub", 0)
    parent_change = pl.pallas_call(
        parent_kernel,
        out_shape=shape(half_count, *block, dtype=BF16),
        scratch_shapes=[
            pltpu.VMEM((half_count, *block), F32),
            pltpu.VMEM((half_count, *block), F32),
            pltpu.VMEM((half_count, *square), F32),
        ],
        name="parent_rows",
    )(parent_weight, kept, received, parent_start)

    whole, scalars = pl.BlockSpec(memory_space=pltpu.VMEM), pl.BlockSpec(memory_space=pltpu.SMEM)
    return pl.pallas_call(
        functools.partial(couple_kernel, groups),
        out_shape=(
            shape(leaf_count, rank_new, points, dtype=BF16),
            shape(leaf_count, leaf_links, rank_new * rank_new, dtype=BF16),
            shape(half_count, parent_links, rank_new * rank_new, dtype=BF16),
        ),
        in_specs=[scalars] * 4 + [whole] * 5,
        out_specs=(whole,) * 3,
        scratch_shapes=[
            pltpu.VMEM((members * leaf_count, *block), BF16),
            pltpu.VMEM((groups * half_count, *block), BF16),
            pltpu.VMEM((leaf_count * leaf_links, *block), BF16),
            pltpu.VMEM((half_count * parent_links, *block), BF16),
            pltpu.VMEM((leaf_links * rank_new // 2, 2 * rank_new), F32),
            pltpu.SemaphoreType.DMA((3,)),
            pltpu.SemaphoreType.DMA((28,)),
            pltpu.SemaphoreType.DMA((28,)),
            pltpu.SemaphoreType.DMA((32,)),
            pltpu.SemaphoreType.DMA((32,)),
        ],
        compiler_params=pltpu.CompilerParams(collective_id=0, has_side_effects=True),
        name="couple",
    )(
        leaf_partner_dev, leaf_partner_slot, parent_partner_group, parent_partner_slot,
        change, parent_change, leaf_bases, leaf_blocks, parent_blocks,
    )


def solution(mesh):
    placed = (
        P(("grp", "sub"), None, None),
        P(("grp", "sub"), None, None),
        P(("grp", "sub"), None, None, None),
        P(("grp", "sub"), None),
        P(("grp", "sub"), None),
        P(("grp", "sub"), None, None, None),
        P(("grp", "sub"), None),
        P(("grp", "sub"), None),
        P(),
        P(),
    )
    return jax.shard_map(
        shards,
        mesh=mesh,
        in_specs=placed,
        out_specs=(
            P(("grp", "sub"), None, None),
            P(("grp", "sub"), None, None),
            P(("grp", "sub"), None, None),
        ),
        check_vma=False,
    )
```

```python
import functools

import jax
import jax.numpy as jnp
from jax import lax
from jax.experimental import pallas as pl
from jax.experimental.pallas import tpu as pltpu
from jax.sharding import PartitionSpec as P

MESH = pl.DeviceIdType.MESH
F32 = jnp.float32
BF16 = jnp.bfloat16
SIDE = 4


def nt(left, right):
    return lax.dot_general(left, right, (((1,), (1,)), ((), ())), preferred_element_type=F32)


def nn(left, right):
    return lax.dot_general(left, right, (((1,), (0,)), ((), ())), preferred_element_type=F32)


def beside(*parts):
    return jnp.concatenate(parts, axis=1)


def above(*parts):
    return jnp.concatenate(parts, axis=0)


def split(values):
    high = values.astype(BF16)
    return high, (values - high.astype(F32)).astype(BF16)


def fold(values):
    width = values.shape[1] // 2
    return values[:, :width] + values[:, width:]


def product(left, right):
    wide = beside(*right)
    return fold(nn(beside(*left), above(wide, wide)))


def product_t(left, right):
    high, low = right
    return fold(nt(beside(*left), above(beside(high, high), beside(low, low))))


def panel(tiles, at):
    full = tiles[0].shape
    rows, width = full[1:]
    half = width // 2
    flat = (full[0] * rows, width)
    place = lax.broadcasted_iota(jnp.int32, full, 1)
    inside = lax.broadcasted_iota(jnp.int32, full, 2) % half - at * rows
    owned = (inside >= 0) & (inside < rows)
    base = lax.broadcasted_iota(jnp.int32, flat, 1) // half * half + at * rows

    def column(values, j):
        picked = jnp.take_along_axis(values.reshape(flat), base + j, axis=1, mode="promise_in_bounds")
        return picked.reshape(full)

    def line(values, j):
        return jnp.broadcast_to(values[:, j : j + 1, :], full)

    tile = tiles[at]
    columns = [column(tile, j) for j in range(rows)]
    tile = jnp.where(owned, jnp.where(inside == place, 1.0, 0.0), tile)
    scale = jnp.zeros(full, F32)
    recip = jnp.zeros(full, F32)
    for k in range(rows):
        inverse = 1.0 / columns[k]
        scale = jnp.where(place == k, lax.rsqrt(columns[k]), scale)
        recip = jnp.where(place == k, inverse, recip)
        if k < rows - 1:
            factor = jnp.where(place > k, columns[k] * line(inverse, k), 0.0)
            for j in range(k + 1, rows):
                columns[j] = columns[j] - factor * line(columns[j], k)
            tile = tile - factor * line(tile, k)
    tiles[at] = jnp.where(inside < rows, tile * scale, 0.0)
    if at + 1 == len(tiles):
        return
    solved = tile * recip
    for k in range(rows - 1, 0, -1):
        solved = solved - jnp.where(place < k, columns[k] * recip, 0.0) * line(solved, k)
    lines = [line(solved, j) for j in range(rows)]
    for i in range(at + 1, len(tiles)):
        old = tiles[i]
        parts = [column(old, j) * lines[j] for j in range(rows)]
        while len(parts) > 1:
            parts = [left + right for left, right in zip(parts[::2], parts[1::2])]
        tiles[i] = jnp.where(owned, 0.0, old) - parts[0]


def eliminate(grams):
    tiles = [grams[:, 8 * i : 8 * i + 8, :] for i in range(grams.shape[1] // 8)]
    for at in range(len(tiles)):
        panel(tiles, at)
    return jnp.concatenate(tiles, axis=1)


def image_of(start, weight):
    terms = split(weight)
    return split(product(split(product(start, terms)), terms))


def diagonal(first, second):
    blank = jnp.zeros_like(first)
    return above(beside(first, blank), beside(blank, second))


def gram_pair(first, second):
    rows = first[0].shape[0]
    left = above(beside(first[0], second[0]), beside(first[1], second[1]))
    right = above(diagonal(first[0], second[0]), diagonal(first[1], second[1]))
    both = fold(nt(left, right))
    return both[:rows] + both[rows:]


def rows_pair(inverses, first, second):
    left = beside(*split(inverses))
    both = 0.0
    for part in range(2):
        block = diagonal(first[part], second[part])
        both = both + nn(left, above(block, block))
    width = both.shape[1] // 2
    return both[:, :width], both[:, width:]


def kernel(
    groups,
    leaf_dev_in, leaf_slot_in, parent_group_in, parent_slot_in,
    leaf_start_ref, parent_start_ref, bases_in, transfers_in, leaf_blocks_in, parent_blocks_in,
    bases_out, leaf_out, parent_out,
    leaf_dev_ref, leaf_slot_ref, parent_group_ref, parent_slot_ref,
    bases_ref, transfers_ref, leaf_blocks_ref, parent_blocks_ref,
    leaves, parents, change, parent_change, half_rows, parent_half_rows, staged,
    weight_high, weight_low, other_weight, kept, sent, received, stacked_high, stacked_low,
    image_high, image_low, grams, parent_image_high, parent_image_low, parent_grams,
    load_sem, pair_send, pair_recv, leaf_send, leaf_recv, ring_send, ring_recv,
):
    count, links = leaf_blocks_ref.shape[:2]
    parent_count, parent_links = parent_blocks_ref.shape[:2]
    rank = change.shape[1]
    part = count // 2
    chunk = parent_count // 2
    sub, grp = lax.axis_index("sub"), lax.axis_index("grp")
    across, along, core = sub // (2 * SIDE), (sub // 2) % SIDE, sub % 2
    member = core

    def site(x, y, c):
        return ((x + SIDE) % SIDE * SIDE + (y + SIDE) % SIDE) * 2 + c

    def near(h, outer, inner):
        if h == 0:
            return site(across + inner, along + outer, core)
        return site(across + outer, along + inner, core)

    outer_at = (along, across)
    inner_at = (across, along)

    def row_start(h, outer):
        return ((h * 2 + core) * SIDE + (outer + SIDE) % SIDE) * SIDE * part

    def block_start(h, outer, inner):
        return row_start(h, outer) + (inner + SIDE) % SIDE * part

    up, down = (grp + 1) % groups, (grp + groups - 1) % groups
    sibling = site(across, along, 1 - core)

    barrier = pltpu.get_barrier_semaphore()
    for target in (near(0, 0, 1), near(0, 0, -1), near(0, 1, 0), near(0, -1, 0), sibling):
        pl.semaphore_signal(barrier, inc=1, device_id={"sub": target}, device_id_type=MESH)
    for target in (up, down):
        pl.semaphore_signal(barrier, inc=1, device_id={"grp": target}, device_id_type=MESH)

    loads = [
        pltpu.make_async_copy(src, dst, load_sem.at[n])
        for n, (src, dst) in enumerate(
            (
                (parent_blocks_in, parent_blocks_ref),
                (leaf_blocks_in, leaf_blocks_ref),
                (transfers_in, transfers_ref),
                (bases_in, bases_ref),
                (leaf_dev_in, leaf_dev_ref),
                (leaf_slot_in, leaf_slot_ref),
                (parent_group_in, parent_group_ref),
                (parent_slot_in, parent_slot_ref),
            )
        )
    ]
    for copy in loads:
        copy.start()

    started = []

    def send_pair(number, src, dst):
        copy = pltpu.make_async_remote_copy(
            src_ref=src,
            dst_ref=dst,
            send_sem=pair_send.at[number],
            recv_sem=pair_recv.at[number],
            device_id={"sub": sibling},
            device_id_type=MESH,
        )
        copy.start()
        started.append(copy)
        return copy

    def send_leaf(number, src, start, size, target):
        copy = pltpu.make_async_remote_copy(
            src_ref=src,
            dst_ref=leaves.at[pl.ds(start, size)],
            send_sem=leaf_send.at[number],
            recv_sem=leaf_recv.at[number],
            device_id={"sub": target},
            device_id_type=MESH,
        )
        copy.start()
        started.append(copy)
        return copy

    def pass_leaf(number, start, size, target):
        return send_leaf(number, leaves.at[pl.ds(start, size)], start, size, target)

    def send_parent(way, step, piece):
        number = (way * (groups // 2) + step) * 2 + piece
        origin = (grp - step + groups) % groups if way == 0 else (grp + step) % groups
        at = origin * parent_count + piece * chunk
        src = parent_change.at[pl.ds(piece * chunk, chunk)] if step == 0 else parents.at[pl.ds(at, chunk)]
        copy = pltpu.make_async_remote_copy(
            src_ref=src,
            dst_ref=parents.at[pl.ds(at, chunk)],
            send_sem=ring_send.at[number],
            recv_sem=ring_recv.at[number],
            device_id={"grp": up if way == 0 else down},
            device_id_type=MESH,
        )
        copy.start()
        started.append(copy)
        return copy

    loads[0].wait()

    @pl.loop(0, parent_count, unroll=3)
    def _(p):
        total = nt(parent_blocks_ref[p, 0], parent_blocks_ref[p, 0])
        for c in range(1, parent_links):
            total = total + nt(parent_blocks_ref[p, c], parent_blocks_ref[p, c])
        weight_high[p], weight_low[p] = split(total)

    loads[1].wait()
    loads[2].wait()
    pl.semaphore_wait(barrier, 7)
    other_sent = send_pair(0, weight_high, other_weight)

    start = split(leaf_start_ref[...])

    def leaf_image(which, p, high, low):
        t = (member + which * (1 - 2 * member)) * part + p
        weight = None
        for c in range(0, links, 2):
            pair = beside(leaf_blocks_ref[t, c], leaf_blocks_ref[t, c + 1])
            weight = nt(pair, pair) if weight is None else weight + nt(pair, pair)
        transfer = transfers_ref[t]
        twice = beside(transfer, transfer)
        carried = nn(transfer, high) if low is None else nn(twice, above(high, low))
        weight = weight + nt(beside(*split(carried)), twice)
        image_high[which * part + p], image_low[which * part + p] = image_of(start, weight)

    @pl.loop(0, part, unroll=3)
    def _(p):
        leaf_image(0, p, weight_high[p], weight_low[p])

    other_sent.wait_recv()

    @pl.loop(0, part, unroll=3)
    def _(p):
        leaf_image(1, p, other_weight[p], None)

    def leaf_terms(which, p):
        return image_high[which * part + p], image_low[which * part + p]

    @pl.loop(0, part, unroll=3)
    def _(p):
        grams[p] = gram_pair(leaf_terms(0, p), leaf_terms(1, p))

    grams[...] = eliminate(grams[...])

    own_start = [block_start(h, outer_at[h], inner_at[h]) for h in range(2)]

    @pl.loop(0, part, unroll=3)
    def _(p):
        both = rows_pair(grams[p], leaf_terms(0, p), leaf_terms(1, p))
        for which in range(2):
            h = member + which * (1 - 2 * member)
            t = h * part + p
            rows = both[which].astype(BF16)
            change[t] = rows
            leaves[own_start[0] + h * (own_start[1] - own_start[0]) + p] = rows
            projected = nn(rows, transfers_ref[t])
            if which == 0:
                kept[p] = projected
            else:
                sent[p] = projected.astype(BF16)

    rows_sent = send_pair(1, sent, received)
    inner_up, inner_down = [], []
    for h in range(2):
        own = change.at[pl.ds(h * part, part)]
        inner_up.append(send_leaf(h * 2, own, own_start[h], part, near(h, 0, 1)))
        inner_down.append(send_leaf(h * 2 + 1, own, own_start[h], part, near(h, 0, -1)))

    loads[3].wait()

    @pl.loop(0, count, unroll=3)
    def _(t):
        bases_out[t] = nt(change[t], bases_ref[t]).astype(BF16)

    rows_sent.wait_recv()
    parent_start = split(parent_start_ref[...])
    first = member == 0

    @pl.loop(0, parent_count, unroll=3)
    def _(p):
        mine, other = kept[p], received[p].astype(F32)
        stacked = split(above(jnp.where(first, mine, other), jnp.where(first, other, mine)))
        stacked_high[p], stacked_low[p] = stacked
        left = product(stacked, (weight_high[p], weight_low[p]))
        gram = product_t(split(left), stacked)
        parent_image_high[p], parent_image_low[p] = image_of(parent_start, gram)

    def parent_terms(p):
        return parent_image_high[p], parent_image_low[p]

    @pl.loop(0, chunk, unroll=3)
    def _(p):
        parent_grams[p] = gram_pair(parent_terms(p), parent_terms(p + chunk))

    for h in range(2):
        inner_up[h].wait_recv()
        inner_down[h].wait_recv()
    second_up, second_down = [], []
    cut = part // 2
    for h in range(2):
        outer, inner = outer_at[h], inner_at[h]
        second_up.append(
            pass_leaf(4 + h * 2, block_start(h, outer, inner - 1), cut, near(h, 0, 1))
        )
        second_down.append(
            pass_leaf(5 + h * 2, block_start(h, outer, inner + 1) + cut, part - cut, near(h, 0, -1))
        )

    parent_grams[...] = eliminate(parent_grams[...])

    @pl.loop(0, chunk, unroll=3)
    def _(p):
        both = rows_pair(parent_grams[p], parent_terms(p), parent_terms(p + chunk))
        for which in range(2):
            q = p + which * chunk
            rows = product(split(both[which]), (stacked_high[q], stacked_low[q])).astype(BF16)
            parent_change[q] = rows
            parents[grp * parent_count + q] = rows

    ring = {}
    for piece in range(2):
        for way in range(2):
            ring[way, 0, piece] = send_parent(way, 0, piece)

    def ring_step(step):
        for piece in range(2):
            for way in range(2):
                if (way, step, piece) not in ring:
                    continue
                ring[way, step, piece].wait_recv()
                if step < groups // 2 - 2 or (step == groups // 2 - 2 and way == piece):
                    ring[way, step + 1, piece] = send_parent(way, step + 1, piece)

    for h in range(2):
        second_up[h].wait_recv()
        second_down[h].wait_recv()
    size = SIDE * part
    cut = size // 2
    rows_up, rows_down, rest_up, rest_down = [], [], [], []
    for h in range(2):
        at = row_start(h, outer_at[h])
        rows_up.append(pass_leaf(8 + h * 6, at, cut, near(h, 1, 0)))
        rows_down.append(pass_leaf(9 + h * 6, at + cut, size - cut, near(h, -1, 0)))
    for h in range(2):
        at = row_start(h, outer_at[h])
        rest_up.append(pass_leaf(10 + h * 6, at + cut, size - cut, near(h, 1, 0)))
        rest_down.append(pass_leaf(11 + h * 6, at, cut, near(h, -1, 0)))
    shared = [pass_leaf(20 + h * 4, row_start(h, outer_at[h]), size, sibling) for h in range(2)]

    row = lax.broadcasted_iota(jnp.int32, (rank, rank), 0)
    column = lax.broadcasted_iota(jnp.int32, (rank, rank), 1)
    low = rank // 2
    order = jnp.where(row < low, 2 * row, 2 * (row - low) + 1)
    shuffle = jnp.where(column == order, 1.0, 0.0).astype(BF16)

    @pl.loop(0, parent_count, unroll=3)
    def _(p):
        mixed = nn(shuffle, parent_change[p]).astype(BF16)
        for c in range(parent_links):
            parent_half_rows[p * parent_links + c] = nn(mixed, parent_blocks_ref[p, c]).astype(BF16)

    def leaf_halves(begin, end):
        @pl.loop(begin, end, unroll=3)
        def _(t):
            mixed = nn(shuffle, change[t]).astype(BF16)
            for c in range(links):
                half_rows[t * links + c] = nn(mixed, leaf_blocks_ref[t, c]).astype(BF16)

    ring_step(0)
    leaf_halves(0, 3)
    ring_step(1)
    leaf_halves(3, 6)
    ring_step(2)
    leaf_halves(6, 9)
    ring_step(3)
    leaf_halves(9, 12)
    last_up, last_down = [], []
    for h in range(2):
        rows_up[h].wait_recv()
        last_up.append(pass_leaf(12 + h * 6, row_start(h, outer_at[h] - 1), cut, near(h, 1, 0)))
        rows_down[h].wait_recv()
        last_down.append(
            pass_leaf(13 + h * 6, row_start(h, outer_at[h] + 1) + cut, size - cut, near(h, -1, 0))
        )
    ring_step(4)
    for h in range(2):
        rest_up[h].wait_recv()
        shared.append(pass_leaf(21 + h * 4, row_start(h, outer_at[h] - 1), size, sibling))
        rest_down[h].wait_recv()
        shared.append(pass_leaf(22 + h * 4, row_start(h, outer_at[h] + 1), size, sibling))
    ring_step(5)
    for h in range(2):
        last_up[h].wait_recv()
        last_down[h].wait_recv()
        shared.append(pass_leaf(23 + h * 4, row_start(h, outer_at[h] + 2), size, sibling))
    ring_step(6)
    for copy in shared:
        copy.wait_recv()
    for copy in loads[4:]:
        copy.wait()

    def couple(half_pair, distant):
        return nt(beside(half_pair[:low], half_pair[low:]), diagonal(distant, distant))

    def flatten(out, at, slot, width):
        for q in range(low):
            rows = staged[slot, pl.ds(q, width, stride=low), :]
            out[at, :, 2 * rank * q : 2 * rank * (q + 1)] = rows.astype(BF16)

    @pl.loop(0, count // 2)
    def _(pair):
        for slot in range(2):
            t = pair * 2 + slot
            for c in range(links):
                place, at = leaf_dev_ref[c, t], leaf_slot_ref[c, t]
                x, y, z = place // (2 * SIDE), place // 2 % SIDE, place % 2
                h = at // part
                outer, inner = y + h * (x - y), x + h * (y - x)
                index = (((h * 2 + z) * SIDE + outer) * SIDE + inner) * part + at - h * part
                staged[slot, low * c : low * (c + 1), :] = couple(half_rows[t * links + c], leaves[index])
        for slot in range(2):
            flatten(leaf_out, pair * 2 + slot, slot, links)

    ring_step(7)

    @pl.loop(0, parent_count // 2)
    def _(pair):
        for slot in range(2):
            p = pair * 2 + slot
            for c in range(parent_links):
                index = parent_group_ref[c, p] * parent_count + parent_slot_ref[c, p]
                staged[slot, low * c : low * (c + 1), :] = couple(
                    parent_half_rows[p * parent_links + c], parents[index]
                )
        for slot in range(2):
            flatten(parent_out, pair * 2 + slot, slot, parent_links)

    for copy in started:
        copy.wait_send()


def shards(
    leaf_bases,
    leaf_transfers,
    leaf_blocks,
    leaf_partner_dev,
    leaf_partner_slot,
    parent_blocks,
    parent_partner_group,
    parent_partner_slot,
    leaf_start,
    parent_start,
):
    leaf_count, leaf_links = leaf_blocks.shape[:2]
    half_count, parent_links = parent_blocks.shape[:2]
    rank_new, rank_old = leaf_start.shape
    points = leaf_bases.shape[1]
    groups, members = lax.axis_size("grp"), lax.axis_size("sub")
    square = (rank_old, rank_old)
    block = (rank_new, rank_old)
    paired = (rank_new, 2 * rank_new)

    def shape(*sizes):
        return jax.ShapeDtypeStruct(sizes, BF16)

    def room(*sizes, dtype=BF16):
        return pltpu.VMEM(sizes, dtype)

    whole, outside = pl.BlockSpec(memory_space=pltpu.VMEM), pl.BlockSpec(memory_space=pl.ANY)
    indices = (leaf_partner_dev.T, leaf_partner_slot.T, parent_partner_group.T, parent_partner_slot.T)
    streams = (leaf_bases, leaf_transfers, leaf_blocks, parent_blocks)
    transfers = (2, 28, 4 * groups // 2)
    return pl.pallas_call(
        functools.partial(kernel, groups),
        out_shape=(
            shape(leaf_count, rank_new, points),
            shape(leaf_count, leaf_links, rank_new * rank_new),
            shape(half_count, parent_links, rank_new * rank_new),
        ),
        in_specs=[outside] * 4 + [whole] * 2 + [outside] * 4,
        out_specs=(whole,) * 3,
        scratch_shapes=[pltpu.SMEM(values.shape, jnp.int32) for values in indices]
        + [room(*values.shape) for values in streams]
        + [
            room(members * leaf_count, *block),
            room(groups * half_count, *block),
            room(leaf_count, *block),
            room(half_count, *block),
            room(leaf_count * leaf_links, *block),
            room(half_count * parent_links, *block),
            room(2, leaf_links * rank_new // 2, 2 * rank_new, dtype=F32),
            room(half_count, *square),
            room(half_count, *square),
            room(half_count, *square),
            room(half_count, *block, dtype=F32),
            room(half_count, *block),
            room(half_count, *block),
            room(half_count, *square),
            room(half_count, *square),
            room(leaf_count, *block),
            room(leaf_count, *block),
            room(leaf_count // 2, *paired, dtype=F32),
            room(half_count, *block),
            room(half_count, *block),
            room(half_count // 2, *paired, dtype=F32),
            pltpu.SemaphoreType.DMA((8,)),
        ]
        + [pltpu.SemaphoreType.DMA((number,)) for number in transfers for _ in range(2)],
        compiler_params=pltpu.CompilerParams(collective_id=0, has_side_effects=True),
        name="recompress",
    )(*indices, leaf_start, parent_start, *streams)


def solution(mesh):
    placed = (
        P(("grp", "sub"), None, None),
        P(("grp", "sub"), None, None),
        P(("grp", "sub"), None, None, None),
        P(("grp", "sub"), None),
        P(("grp", "sub"), None),
        P(("grp", "sub"), None, None, None),
        P(("grp", "sub"), None),
        P(("grp", "sub"), None),
        P(),
        P(),
    )
    return jax.shard_map(
        shards,
        mesh=mesh,
        in_specs=placed,
        out_specs=(
            P(("grp", "sub"), None, None),
            P(("grp", "sub"), None, None),
            P(("grp", "sub"), None, None),
        ),
        check_vma=False,
    )
```

```python
import functools

import jax
import jax.numpy as jnp
from jax import lax
from jax.experimental import pallas as pl
from jax.experimental.pallas import tpu as pltpu
from jax.sharding import PartitionSpec as P

MESH = pl.DeviceIdType.MESH
F32 = jnp.float32
BF16 = jnp.bfloat16
SIDE = 4


def nt(left, right):
    return lax.dot_general(left, right, (((1,), (1,)), ((), ())), preferred_element_type=F32)


def nn(left, right):
    return lax.dot_general(left, right, (((1,), (0,)), ((), ())), preferred_element_type=F32)


def beside(*parts):
    return jnp.concatenate(parts, axis=1)


def above(*parts):
    return jnp.concatenate(parts, axis=0)


def split(values):
    high = values.astype(BF16)
    return high, (values - high.astype(F32)).astype(BF16)


def fold(values):
    width = values.shape[1] // 2
    return values[:, :width] + values[:, width:]


def product(left, right):
    wide = beside(*right)
    return fold(nn(beside(*left), above(wide, wide)))


def product_t(left, right):
    high, low = right
    return fold(nt(beside(*left), above(beside(high, high), beside(low, low))))


def panel(tiles, at):
    full = tiles[0].shape
    rows, width = full[1:]
    half = width // 2
    flat = (full[0] * rows, width)
    place = lax.broadcasted_iota(jnp.int32, full, 1)
    inside = lax.broadcasted_iota(jnp.int32, full, 2) % half - at * rows
    owned = (inside >= 0) & (inside < rows)
    base = lax.broadcasted_iota(jnp.int32, flat, 1) // half * half + at * rows

    def column(values, j):
        picked = jnp.take_along_axis(values.reshape(flat), base + j, axis=1, mode="promise_in_bounds")
        return picked.reshape(full)

    def line(values, j):
        return jnp.broadcast_to(values[:, j : j + 1, :], full)

    tile = tiles[at]
    columns = [column(tile, j) for j in range(rows)]
    tile = jnp.where(owned, jnp.where(inside == place, 1.0, 0.0), tile)
    scale = jnp.zeros(full, F32)
    recip = jnp.zeros(full, F32)
    for k in range(rows):
        inverse = 1.0 / columns[k]
        scale = jnp.where(place == k, lax.rsqrt(columns[k]), scale)
        recip = jnp.where(place == k, inverse, recip)
        if k < rows - 1:
            factor = jnp.where(place > k, columns[k] * line(inverse, k), 0.0)
            for j in range(k + 1, rows):
                columns[j] = columns[j] - factor * line(columns[j], k)
            tile = tile - factor * line(tile, k)
    tiles[at] = jnp.where(inside < rows, tile * scale, 0.0)
    if at + 1 == len(tiles):
        return
    solved = tile * recip
    for k in range(rows - 1, 0, -1):
        solved = solved - jnp.where(place < k, columns[k] * recip, 0.0) * line(solved, k)
    lines = [line(solved, j) for j in range(rows)]
    for i in range(at + 1, len(tiles)):
        old = tiles[i]
        parts = [column(old, j) * lines[j] for j in range(rows)]
        while len(parts) > 1:
            parts = [left + right for left, right in zip(parts[::2], parts[1::2])]
        tiles[i] = jnp.where(owned, 0.0, old) - parts[0]


def eliminate(grams):
    tiles = [grams[:, 8 * i : 8 * i + 8, :] for i in range(grams.shape[1] // 8)]
    for at in range(len(tiles)):
        panel(tiles, at)
    return jnp.concatenate(tiles, axis=1)


def image_of(start, weight):
    terms = split(weight)
    return split(product(split(product(start, terms)), terms))


def diagonal(first, second):
    blank = jnp.zeros_like(first)
    return above(beside(first, blank), beside(blank, second))


def gram_pair(first, second):
    rows = first[0].shape[0]
    left = above(beside(first[0], second[0]), beside(first[1], second[1]))
    right = above(diagonal(first[0], second[0]), diagonal(first[1], second[1]))
    both = fold(nt(left, right))
    return both[:rows] + both[rows:]


def rows_pair(inverses, first, second):
    left = beside(*split(inverses))
    both = 0.0
    for part in range(2):
        block = diagonal(first[part], second[part])
        both = both + nn(left, above(block, block))
    width = both.shape[1] // 2
    return both[:, :width], both[:, width:]


def kernel(
    groups,
    leaf_dev_in, leaf_slot_in, parent_group_in, parent_slot_in,
    leaf_start_ref, parent_start_ref, bases_in, transfers_in, leaf_blocks_in, parent_blocks_in,
    bases_out, leaf_out, parent_out,
    leaf_dev_ref, leaf_slot_ref, parent_group_ref, parent_slot_ref,
    bases_ref, transfers_ref, leaf_blocks_ref, parent_blocks_ref,
    leaves, parents, change, parent_change, half_rows, parent_half_rows, staged,
    weight_high, weight_low, other_weight, kept, sent, received, stacked_high, stacked_low,
    image_high, image_low, grams, parent_image_high, parent_image_low, parent_grams,
    load_sem, pair_send, pair_recv, leaf_send, leaf_recv, ring_send, ring_recv,
):
    count, links = leaf_blocks_ref.shape[:2]
    parent_count, parent_links = parent_blocks_ref.shape[:2]
    rank = change.shape[1]
    part = count // 2
    chunk = parent_count // 2
    sub, grp = lax.axis_index("sub"), lax.axis_index("grp")
    across, along, core = sub // (2 * SIDE), (sub // 2) % SIDE, sub % 2
    member = core

    def site(x, y, c):
        return ((x + SIDE) % SIDE * SIDE + (y + SIDE) % SIDE) * 2 + c

    def near(h, outer, inner):
        if h == 0:
            return site(across + inner, along + outer, core)
        return site(across + outer, along + inner, core)

    outer_at = (along, across)
    inner_at = (across, along)

    def row_start(h, outer):
        return ((h * 2 + core) * SIDE + (outer + SIDE) % SIDE) * SIDE * part

    def block_start(h, outer, inner):
        return row_start(h, outer) + (inner + SIDE) % SIDE * part

    up, down = (grp + 1) % groups, (grp + groups - 1) % groups
    sibling = site(across, along, 1 - core)

    barrier = pltpu.get_barrier_semaphore()
    for target in (near(0, 0, 1), near(0, 0, -1), near(0, 1, 0), near(0, -1, 0), sibling):
        pl.semaphore_signal(barrier, inc=1, device_id={"sub": target}, device_id_type=MESH)
    for target in (up, down):
        pl.semaphore_signal(barrier, inc=1, device_id={"grp": target}, device_id_type=MESH)

    loads = [
        pltpu.make_async_copy(src, dst, load_sem.at[n])
        for n, (src, dst) in enumerate(
            (
                (parent_blocks_in, parent_blocks_ref),
                (leaf_blocks_in, leaf_blocks_ref),
                (transfers_in, transfers_ref),
                (bases_in, bases_ref),
                (leaf_dev_in, leaf_dev_ref),
                (leaf_slot_in, leaf_slot_ref),
                (parent_group_in, parent_group_ref),
                (parent_slot_in, parent_slot_ref),
            )
        )
    ]
    for copy in loads:
        copy.start()

    started = []

    def send_pair(number, src, dst):
        copy = pltpu.make_async_remote_copy(
            src_ref=src,
            dst_ref=dst,
            send_sem=pair_send.at[number],
            recv_sem=pair_recv.at[number],
            device_id={"sub": sibling},
            device_id_type=MESH,
        )
        copy.start()
        started.append(copy)
        return copy

    def send_leaf(number, src, start, size, target):
        copy = pltpu.make_async_remote_copy(
            src_ref=src,
            dst_ref=leaves.at[pl.ds(start, size)],
            send_sem=leaf_send.at[number],
            recv_sem=leaf_recv.at[number],
            device_id={"sub": target},
            device_id_type=MESH,
        )
        copy.start()
        started.append(copy)
        return copy

    def pass_leaf(number, start, size, target):
        return send_leaf(number, leaves.at[pl.ds(start, size)], start, size, target)

    def send_parent(way, step, piece):
        number = (way * (groups // 2) + step) * 2 + piece
        origin = (grp - step + groups) % groups if way == 0 else (grp + step) % groups
        at = origin * parent_count + piece * chunk
        src = parent_change.at[pl.ds(piece * chunk, chunk)] if step == 0 else parents.at[pl.ds(at, chunk)]
        copy = pltpu.make_async_remote_copy(
            src_ref=src,
            dst_ref=parents.at[pl.ds(at, chunk)],
            send_sem=ring_send.at[number],
            recv_sem=ring_recv.at[number],
            device_id={"grp": up if way == 0 else down},
            device_id_type=MESH,
        )
        copy.start()
        started.append(copy)
        return copy

    loads[0].wait()

    @pl.loop(0, parent_count, unroll=3)
    def _(p):
        total = nt(parent_blocks_ref[p, 0], parent_blocks_ref[p, 0])
        for c in range(1, parent_links):
            total = total + nt(parent_blocks_ref[p, c], parent_blocks_ref[p, c])
        weight_high[p], weight_low[p] = split(total)

    loads[1].wait()
    loads[2].wait()
    pl.semaphore_wait(barrier, 7)
    other_sent = send_pair(0, weight_high, other_weight)

    start = split(leaf_start_ref[...])

    def leaf_image(which, p, high, low):
        t = (member + which * (1 - 2 * member)) * part + p
        weight = None
        for c in range(0, links, 2):
            pair = beside(leaf_blocks_ref[t, c], leaf_blocks_ref[t, c + 1])
            weight = nt(pair, pair) if weight is None else weight + nt(pair, pair)
        transfer = transfers_ref[t]
        twice = beside(transfer, transfer)
        carried = nn(transfer, high) if low is None else nn(twice, above(high, low))
        weight = weight + nt(beside(*split(carried)), twice)
        image_high[which * part + p], image_low[which * part + p] = image_of(start, weight)

    @pl.loop(0, part, unroll=3)
    def _(p):
        leaf_image(0, p, weight_high[p], weight_low[p])

    other_sent.wait_recv()

    @pl.loop(0, part, unroll=3)
    def _(p):
        leaf_image(1, p, other_weight[p], None)

    def leaf_terms(which, p):
        return image_high[which * part + p], image_low[which * part + p]

    @pl.loop(0, part, unroll=3)
    def _(p):
        grams[p] = gram_pair(leaf_terms(0, p), leaf_terms(1, p))

    grams[...] = eliminate(grams[...])

    own_start = [block_start(h, outer_at[h], inner_at[h]) for h in range(2)]

    @pl.loop(0, part, unroll=3)
    def _(p):
        both = rows_pair(grams[p], leaf_terms(0, p), leaf_terms(1, p))
        for which in range(2):
            h = member + which * (1 - 2 * member)
            t = h * part + p
            rows = both[which].astype(BF16)
            change[t] = rows
            leaves[own_start[0] + h * (own_start[1] - own_start[0]) + p] = rows
            projected = nn(rows, transfers_ref[t])
            if which == 0:
                kept[p] = projected
            else:
                sent[p] = projected.astype(BF16)

    rows_sent = send_pair(1, sent, received)
    inner_up, inner_down = [], []
    for h in range(2):
        own = change.at[pl.ds(h * part, part)]
        inner_up.append(send_leaf(h * 2, own, own_start[h], part, near(h, 0, 1)))
        inner_down.append(send_leaf(h * 2 + 1, own, own_start[h], part, near(h, 0, -1)))

    loads[3].wait()

    @pl.loop(0, count, unroll=3)
    def _(t):
        bases_out[t] = nt(change[t], bases_ref[t]).astype(BF16)

    rows_sent.wait_recv()
    parent_start = split(parent_start_ref[...])
    first = member == 0

    @pl.loop(0, parent_count, unroll=3)
    def _(p):
        mine, other = kept[p], received[p].astype(F32)
        stacked = split(above(jnp.where(first, mine, other), jnp.where(first, other, mine)))
        stacked_high[p], stacked_low[p] = stacked
        left = product(stacked, (weight_high[p], weight_low[p]))
        gram = product_t(split(left), stacked)
        parent_image_high[p], parent_image_low[p] = image_of(parent_start, gram)

    def parent_terms(p):
        return parent_image_high[p], parent_image_low[p]

    @pl.loop(0, chunk, unroll=3)
    def _(p):
        parent_grams[p] = gram_pair(parent_terms(p), parent_terms(p + chunk))

    for h in range(2):
        inner_up[h].wait_recv()
        inner_down[h].wait_recv()
    second_up, second_down = [], []
    cut = part // 2
    for h in range(2):
        outer, inner = outer_at[h], inner_at[h]
        second_up.append(
            pass_leaf(4 + h * 2, block_start(h, outer, inner - 1), cut, near(h, 0, 1))
        )
        second_down.append(
            pass_leaf(5 + h * 2, block_start(h, outer, inner + 1) + cut, part - cut, near(h, 0, -1))
        )

    parent_grams[...] = eliminate(parent_grams[...])

    @pl.loop(0, chunk, unroll=3)
    def _(p):
        both = rows_pair(parent_grams[p], parent_terms(p), parent_terms(p + chunk))
        for which in range(2):
            q = p + which * chunk
            rows = product(split(both[which]), (stacked_high[q], stacked_low[q])).astype(BF16)
            parent_change[q] = rows
            parents[grp * parent_count + q] = rows

    ring = {}
    for piece in range(2):
        for way in range(2):
            ring[way, 0, piece] = send_parent(way, 0, piece)

    def ring_step(step):
        for piece in range(2):
            for way in range(2):
                if (way, step, piece) not in ring:
                    continue
                ring[way, step, piece].wait_recv()
                if step < groups // 2 - 2 or (step == groups // 2 - 2 and way == piece):
                    ring[way, step + 1, piece] = send_parent(way, step + 1, piece)

    for h in range(2):
        second_up[h].wait_recv()
        second_down[h].wait_recv()
    size = SIDE * part
    cut = size // 2
    rows_up, rows_down, rest_up, rest_down = [], [], [], []
    for h in range(2):
        at = row_start(h, outer_at[h])
        rows_up.append(pass_leaf(8 + h * 6, at, cut, near(h, 1, 0)))
        rows_down.append(pass_leaf(9 + h * 6, at + cut, size - cut, near(h, -1, 0)))
    for h in range(2):
        at = row_start(h, outer_at[h])
        rest_up.append(pass_leaf(10 + h * 6, at + cut, size - cut, near(h, 1, 0)))
        rest_down.append(pass_leaf(11 + h * 6, at, cut, near(h, -1, 0)))
    shared = [pass_leaf(20 + h * 4, row_start(h, outer_at[h]), size, sibling) for h in range(2)]

    row = lax.broadcasted_iota(jnp.int32, (rank, rank), 0)
    column = lax.broadcasted_iota(jnp.int32, (rank, rank), 1)
    low = rank // 2
    order = jnp.where(row < low, 2 * row, 2 * (row - low) + 1)
    shuffle = jnp.where(column == order, 1.0, 0.0).astype(BF16)

    @pl.loop(0, parent_count, unroll=3)
    def _(p):
        mixed = nn(shuffle, parent_change[p]).astype(BF16)
        for c in range(parent_links):
            parent_half_rows[p * parent_links + c] = nn(mixed, parent_blocks_ref[p, c]).astype(BF16)

    def leaf_halves(begin, end):
        @pl.loop(begin, end, unroll=3)
        def _(t):
            mixed = nn(shuffle, change[t]).astype(BF16)
            for c in range(links):
                half_rows[t * links + c] = nn(mixed, leaf_blocks_ref[t, c]).astype(BF16)

    ring_step(0)
    leaf_halves(0, 3)
    ring_step(1)
    leaf_halves(3, 6)
    ring_step(2)
    leaf_halves(6, 9)
    ring_step(3)
    leaf_halves(9, 12)
    last_up, last_down = [], []
    for h in range(2):
        rows_up[h].wait_recv()
        last_up.append(pass_leaf(12 + h * 6, row_start(h, outer_at[h] - 1), cut, near(h, 1, 0)))
        rows_down[h].wait_recv()
        last_down.append(
            pass_leaf(13 + h * 6, row_start(h, outer_at[h] + 1) + cut, size - cut, near(h, -1, 0))
        )
    ring_step(4)
    for h in range(2):
        rest_up[h].wait_recv()
        shared.append(pass_leaf(21 + h * 4, row_start(h, outer_at[h] - 1), size, sibling))
        rest_down[h].wait_recv()
        shared.append(pass_leaf(22 + h * 4, row_start(h, outer_at[h] + 1), size, sibling))
    ring_step(5)
    for h in range(2):
        last_up[h].wait_recv()
        last_down[h].wait_recv()
        shared.append(pass_leaf(23 + h * 4, row_start(h, outer_at[h] + 2), size, sibling))
    ring_step(6)
    for copy in shared:
        copy.wait_recv()
    for copy in loads[4:]:
        copy.wait()

    def couple(half_pair, distant):
        return nt(beside(half_pair[:low], half_pair[low:]), diagonal(distant, distant))

    def flatten(out, at, slot, width):
        for q in range(low):
            rows = staged[slot, pl.ds(q, width, stride=low), :]
            out[at, :, 2 * rank * q : 2 * rank * (q + 1)] = rows.astype(BF16)

    @pl.loop(0, count // 2)
    def _(pair):
        for slot in range(2):
            t = pair * 2 + slot
            for c in range(links):
                place, at = leaf_dev_ref[c, t], leaf_slot_ref[c, t]
                x, y, z = place // (2 * SIDE), place // 2 % SIDE, place % 2
                h = at // part
                outer, inner = y + h * (x - y), x + h * (y - x)
                index = (((h * 2 + z) * SIDE + outer) * SIDE + inner) * part + at - h * part
                staged[slot, low * c : low * (c + 1), :] = couple(half_rows[t * links + c], leaves[index])
        for slot in range(2):
            flatten(leaf_out, pair * 2 + slot, slot, links)

    ring_step(7)

    @pl.loop(0, parent_count // 2)
    def _(pair):
        for slot in range(2):
            p = pair * 2 + slot
            for c in range(parent_links):
                index = parent_group_ref[c, p] * parent_count + parent_slot_ref[c, p]
                staged[slot, low * c : low * (c + 1), :] = couple(
                    parent_half_rows[p * parent_links + c], parents[index]
                )
        for slot in range(2):
            flatten(parent_out, pair * 2 + slot, slot, parent_links)

    for copy in started:
        copy.wait_send()


def shards(
    leaf_bases,
    leaf_transfers,
    leaf_blocks,
    leaf_partner_dev,
    leaf_partner_slot,
    parent_blocks,
    parent_partner_group,
    parent_partner_slot,
    leaf_start,
    parent_start,
):
    leaf_count, leaf_links = leaf_blocks.shape[:2]
    half_count, parent_links = parent_blocks.shape[:2]
    rank_new, rank_old = leaf_start.shape
    points = leaf_bases.shape[1]
    groups, members = lax.axis_size("grp"), lax.axis_size("sub")
    square = (rank_old, rank_old)
    block = (rank_new, rank_old)
    paired = (rank_new, 2 * rank_new)

    def shape(*sizes):
        return pltpu.VMEM(sizes, BF16)

    def room(*sizes, dtype=BF16):
        return pltpu.VMEM(sizes, dtype)

    whole, outside = pl.BlockSpec(memory_space=pltpu.VMEM), pl.BlockSpec(memory_space=pl.ANY)
    indices = (leaf_partner_dev.T, leaf_partner_slot.T, parent_partner_group.T, parent_partner_slot.T)
    streams = (leaf_bases, leaf_transfers, leaf_blocks, parent_blocks)
    transfers = (2, 28, 4 * groups // 2)
    return pl.pallas_call(
        functools.partial(kernel, groups),
        out_shape=(
            shape(leaf_count, rank_new, points),
            shape(leaf_count, leaf_links, rank_new * rank_new),
            shape(half_count, parent_links, rank_new * rank_new),
        ),
        in_specs=[outside] * 4 + [whole] * 2 + [outside] * 4,
        out_specs=(whole,) * 3,
        scratch_shapes=[pltpu.SMEM(values.shape, jnp.int32) for values in indices]
        + [room(*values.shape) for values in streams]
        + [
            room(members * leaf_count, *block),
            room(groups * half_count, *block),
            room(leaf_count, *block),
            room(half_count, *block),
            room(leaf_count * leaf_links, *block),
            room(half_count * parent_links, *block),
            room(2, leaf_links * rank_new // 2, 2 * rank_new, dtype=F32),
            room(half_count, *square),
            room(half_count, *square),
            room(half_count, *square),
            room(half_count, *block, dtype=F32),
            room(half_count, *block),
            room(half_count, *block),
            room(half_count, *square),
            room(half_count, *square),
            room(leaf_count, *block),
            room(leaf_count, *block),
            room(leaf_count // 2, *paired, dtype=F32),
            room(half_count, *block),
            room(half_count, *block),
            room(half_count // 2, *paired, dtype=F32),
            pltpu.SemaphoreType.DMA((8,)),
        ]
        + [pltpu.SemaphoreType.DMA((number,)) for number in transfers for _ in range(2)],
        compiler_params=pltpu.CompilerParams(collective_id=0, has_side_effects=True),
        name="recompress",
    )(*indices, leaf_start, parent_start, *streams)


def solution(mesh):
    placed = (
        P(("grp", "sub"), None, None),
        P(("grp", "sub"), None, None),
        P(("grp", "sub"), None, None, None),
        P(("grp", "sub"), None),
        P(("grp", "sub"), None),
        P(("grp", "sub"), None, None, None),
        P(("grp", "sub"), None),
        P(("grp", "sub"), None),
        P(),
        P(),
    )
    return jax.shard_map(
        shards,
        mesh=mesh,
        in_specs=placed,
        out_specs=(
            P(("grp", "sub"), None, None),
            P(("grp", "sub"), None, None),
            P(("grp", "sub"), None, None),
        ),
        check_vma=False,
    )
```

```python
import functools

import jax
import jax.numpy as jnp
from jax import lax
from jax.experimental import pallas as pl
from jax.experimental.pallas import tpu as pltpu
from jax.sharding import PartitionSpec as P

MESH = pl.DeviceIdType.MESH
F32 = jnp.float32
BF16 = jnp.bfloat16
SIDE = 4


def nt(left, right):
    return lax.dot_general(left, right, (((1,), (1,)), ((), ())), preferred_element_type=F32)


def nn(left, right):
    return lax.dot_general(left, right, (((1,), (0,)), ((), ())), preferred_element_type=F32)


def beside(*parts):
    return jnp.concatenate(parts, axis=1)


def above(*parts):
    return jnp.concatenate(parts, axis=0)


def split(values):
    high = values.astype(BF16)
    return high, (values - high.astype(F32)).astype(BF16)


def fold(values):
    width = values.shape[1] // 2
    return values[:, :width] + values[:, width:]


def product(left, right):
    wide = beside(*right)
    return fold(nn(beside(*left), above(wide, wide)))


def product_t(left, right):
    high, low = right
    return fold(nt(beside(*left), above(beside(high, high), beside(low, low))))


def panel(tiles, at):
    full = tiles[0].shape
    rows, width = full[1:]
    half = width // 2
    flat = (full[0] * rows, width)
    place = lax.broadcasted_iota(jnp.int32, full, 1)
    inside = lax.broadcasted_iota(jnp.int32, full, 2) % half - at * rows
    owned = (inside >= 0) & (inside < rows)
    base = lax.broadcasted_iota(jnp.int32, flat, 1) // half * half + at * rows

    def column(values, j):
        picked = jnp.take_along_axis(values.reshape(flat), base + j, axis=1, mode="promise_in_bounds")
        return picked.reshape(full)

    def line(values, j):
        return jnp.broadcast_to(values[:, j : j + 1, :], full)

    tile = tiles[at]
    columns = [column(tile, j) for j in range(rows)]
    tile = jnp.where(owned, jnp.where(inside == place, 1.0, 0.0), tile)
    scale = jnp.zeros(full, F32)
    recip = jnp.zeros(full, F32)
    for k in range(rows):
        inverse = 1.0 / columns[k]
        scale = jnp.where(place == k, lax.rsqrt(columns[k]), scale)
        recip = jnp.where(place == k, inverse, recip)
        if k < rows - 1:
            factor = jnp.where(place > k, columns[k] * line(inverse, k), 0.0)
            for j in range(k + 1, rows):
                columns[j] = columns[j] - factor * line(columns[j], k)
            tile = tile - factor * line(tile, k)
    tiles[at] = jnp.where(inside < rows, tile * scale, 0.0)
    if at + 1 == len(tiles):
        return
    solved = tile * recip
    for k in range(rows - 1, 0, -1):
        solved = solved - jnp.where(place < k, columns[k] * recip, 0.0) * line(solved, k)
    lines = [line(solved, j) for j in range(rows)]
    for i in range(at + 1, len(tiles)):
        old = tiles[i]
        parts = [column(old, j) * lines[j] for j in range(rows)]
        while len(parts) > 1:
            parts = [left + right for left, right in zip(parts[::2], parts[1::2])]
        tiles[i] = jnp.where(owned, 0.0, old) - parts[0]


def eliminate(grams):
    tiles = [grams[:, 8 * i : 8 * i + 8, :] for i in range(grams.shape[1] // 8)]
    for at in range(len(tiles)):
        panel(tiles, at)
    return jnp.concatenate(tiles, axis=1)


def image_of(start, weight):
    terms = split(weight)
    return split(product(split(product(start, terms)), terms))


def diagonal(first, second):
    blank = jnp.zeros_like(first)
    return above(beside(first, blank), beside(blank, second))


def gram_pair(first, second):
    rows = first[0].shape[0]
    left = above(beside(first[0], second[0]), beside(first[1], second[1]))
    right = above(diagonal(first[0], second[0]), diagonal(first[1], second[1]))
    both = fold(nt(left, right))
    return both[:rows] + both[rows:]


def rows_pair(inverses, first, second):
    left = beside(*split(inverses))
    both = 0.0
    for part in range(2):
        block = diagonal(first[part], second[part])
        both = both + nn(left, above(block, block))
    width = both.shape[1] // 2
    return both[:, :width], both[:, width:]


def kernel(
    groups,
    leaf_dev_in, leaf_slot_in, parent_group_in, parent_slot_in,
    leaf_start_ref, parent_start_ref, bases_in, transfers_in, leaf_blocks_in, parent_blocks_in,
    bases_out, leaf_out, parent_out,
    leaf_dev_ref, leaf_slot_ref, parent_group_ref, parent_slot_ref,
    bases_ref, transfers_ref, leaf_blocks_ref, parent_blocks_ref,
    leaves, parents, change, parent_change, half_rows, parent_half_rows, staged,
    weight_high, weight_low, other_weight, kept, sent, received, stacked_high, stacked_low,
    image_high, image_low, grams, parent_image_high, parent_image_low, parent_grams,
    load_sem, pair_send, pair_recv, leaf_send, leaf_recv, ring_send, ring_recv,
):
    count, links = leaf_blocks_ref.shape[:2]
    parent_count, parent_links = parent_blocks_ref.shape[:2]
    rank = change.shape[1]
    part = count // 2
    chunk = parent_count // 2
    pieces = 3
    share = parent_count // pieces
    sub, grp = lax.axis_index("sub"), lax.axis_index("grp")
    across, along, core = sub // (2 * SIDE), (sub // 2) % SIDE, sub % 2
    member = core

    def site(x, y, c):
        return ((x + SIDE) % SIDE * SIDE + (y + SIDE) % SIDE) * 2 + c

    def near(h, outer, inner):
        if h == 0:
            return site(across + inner, along + outer, core)
        return site(across + outer, along + inner, core)

    outer_at = (along, across)
    inner_at = (across, along)

    def row_start(h, outer):
        return ((h * 2 + core) * SIDE + (outer + SIDE) % SIDE) * SIDE * part

    def block_start(h, outer, inner):
        return row_start(h, outer) + (inner + SIDE) % SIDE * part

    up, down = (grp + 1) % groups, (grp + groups - 1) % groups
    sibling = site(across, along, 1 - core)

    barrier = pltpu.get_barrier_semaphore()
    for target in (near(0, 0, 1), near(0, 0, -1), near(0, 1, 0), near(0, -1, 0), sibling):
        pl.semaphore_signal(barrier, inc=1, device_id={"sub": target}, device_id_type=MESH)
    for target in (up, down):
        pl.semaphore_signal(barrier, inc=1, device_id={"grp": target}, device_id_type=MESH)

    loads = [
        pltpu.make_async_copy(src, dst, load_sem.at[n])
        for n, (src, dst) in enumerate(
            (
                (parent_blocks_in, parent_blocks_ref),
                (leaf_blocks_in, leaf_blocks_ref),
                (transfers_in, transfers_ref),
                (bases_in, bases_ref),
                (leaf_dev_in, leaf_dev_ref),
                (leaf_slot_in, leaf_slot_ref),
                (parent_group_in, parent_group_ref),
                (parent_slot_in, parent_slot_ref),
            )
        )
    ]
    for copy in loads:
        copy.start()

    started = []

    def send_pair(number, src, dst):
        copy = pltpu.make_async_remote_copy(
            src_ref=src,
            dst_ref=dst,
            send_sem=pair_send.at[number],
            recv_sem=pair_recv.at[number],
            device_id={"sub": sibling},
            device_id_type=MESH,
        )
        copy.start()
        started.append(copy)
        return copy

    def send_leaf(number, src, start, size, target):
        copy = pltpu.make_async_remote_copy(
            src_ref=src,
            dst_ref=leaves.at[pl.ds(start, size)],
            send_sem=leaf_send.at[number],
            recv_sem=leaf_recv.at[number],
            device_id={"sub": target},
            device_id_type=MESH,
        )
        copy.start()
        started.append(copy)
        return copy

    def pass_leaf(number, start, size, target):
        return send_leaf(number, leaves.at[pl.ds(start, size)], start, size, target)

    def send_parent(way, step, piece):
        number = (way * (groups // 2) + step) * pieces + piece
        origin = (grp - step + groups) % groups if way == 0 else (grp + step) % groups
        at = origin * parent_count + piece * share
        src = parent_change.at[pl.ds(piece * share, share)] if step == 0 else parents.at[pl.ds(at, share)]
        copy = pltpu.make_async_remote_copy(
            src_ref=src,
            dst_ref=parents.at[pl.ds(at, share)],
            send_sem=ring_send.at[number],
            recv_sem=ring_recv.at[number],
            device_id={"grp": up if way == 0 else down},
            device_id_type=MESH,
        )
        copy.start()
        started.append(copy)
        return copy

    loads[0].wait()

    @pl.loop(0, parent_count, unroll=6)
    def _(p):
        total = nt(parent_blocks_ref[p, 0], parent_blocks_ref[p, 0])
        for c in range(1, parent_links):
            total = total + nt(parent_blocks_ref[p, c], parent_blocks_ref[p, c])
        weight_high[p], weight_low[p] = split(total)

    loads[1].wait()
    loads[2].wait()
    pl.semaphore_wait(barrier, 7)
    other_sent = send_pair(0, weight_high, other_weight)

    start = split(leaf_start_ref[...])

    def leaf_image(which, p, high, low):
        t = (member + which * (1 - 2 * member)) * part + p
        weight = None
        for c in range(0, links, 2):
            pair = beside(leaf_blocks_ref[t, c], leaf_blocks_ref[t, c + 1])
            weight = nt(pair, pair) if weight is None else weight + nt(pair, pair)
        transfer = transfers_ref[t]
        twice = beside(transfer, transfer)
        carried = nn(transfer, high) if low is None else nn(twice, above(high, low))
        weight = weight + nt(beside(*split(carried)), twice)
        image_high[which * part + p], image_low[which * part + p] = image_of(start, weight)

    @pl.loop(0, part, unroll=6)
    def _(p):
        leaf_image(0, p, weight_high[p], weight_low[p])

    other_sent.wait_recv()

    @pl.loop(0, part, unroll=6)
    def _(p):
        leaf_image(1, p, other_weight[p], None)

    def leaf_terms(which, p):
        return image_high[which * part + p], image_low[which * part + p]

    @pl.loop(0, part, unroll=6)
    def _(p):
        grams[p] = gram_pair(leaf_terms(0, p), leaf_terms(1, p))

    grams[...] = eliminate(grams[...])

    own_start = [block_start(h, outer_at[h], inner_at[h]) for h in range(2)]

    @pl.loop(0, part, unroll=6)
    def _(p):
        both = rows_pair(grams[p], leaf_terms(0, p), leaf_terms(1, p))
        for which in range(2):
            h = member + which * (1 - 2 * member)
            t = h * part + p
            rows = both[which].astype(BF16)
            change[t] = rows
            leaves[own_start[0] + h * (own_start[1] - own_start[0]) + p] = rows
            projected = nn(rows, transfers_ref[t])
            if which == 0:
                kept[p] = projected
            else:
                sent[p] = projected.astype(BF16)

    rows_sent = send_pair(1, sent, received)
    inner_up, inner_down = [], []
    for h in range(2):
        own = change.at[pl.ds(h * part, part)]
        inner_up.append(send_leaf(h * 2, own, own_start[h], part, near(h, 0, 1)))
        inner_down.append(send_leaf(h * 2 + 1, own, own_start[h], part, near(h, 0, -1)))

    loads[3].wait()

    @pl.loop(0, count, unroll=6)
    def _(t):
        bases_out[t] = nt(change[t], bases_ref[t]).astype(BF16)

    rows_sent.wait_recv()
    parent_start = split(parent_start_ref[...])
    first = member == 0

    @pl.loop(0, parent_count, unroll=6)
    def _(p):
        mine, other = kept[p], received[p].astype(F32)
        stacked = split(above(jnp.where(first, mine, other), jnp.where(first, other, mine)))
        stacked_high[p], stacked_low[p] = stacked
        left = product(stacked, (weight_high[p], weight_low[p]))
        gram = product_t(split(left), stacked)
        parent_image_high[p], parent_image_low[p] = image_of(parent_start, gram)

    def parent_terms(p):
        return parent_image_high[p], parent_image_low[p]

    @pl.loop(0, chunk, unroll=3)
    def _(p):
        parent_grams[p] = gram_pair(parent_terms(p), parent_terms(p + chunk))

    for h in range(2):
        inner_up[h].wait_recv()
        inner_down[h].wait_recv()
    second_up, second_down = [], []
    cut = part // 2
    for h in range(2):
        outer, inner = outer_at[h], inner_at[h]
        second_up.append(
            pass_leaf(4 + h * 2, block_start(h, outer, inner - 1), cut, near(h, 0, 1))
        )
        second_down.append(
            pass_leaf(5 + h * 2, block_start(h, outer, inner + 1) + cut, part - cut, near(h, 0, -1))
        )

    parent_grams[...] = eliminate(parent_grams[...])

    @pl.loop(0, chunk, unroll=3)
    def _(p):
        both = rows_pair(parent_grams[p], parent_terms(p), parent_terms(p + chunk))
        for which in range(2):
            q = p + which * chunk
            rows = product(split(both[which]), (stacked_high[q], stacked_low[q])).astype(BF16)
            parent_change[q] = rows
            parents[grp * parent_count + q] = rows

    ring = {}
    for piece in range(pieces):
        for way in range(2):
            ring[way, 0, piece] = send_parent(way, 0, piece)

    def ring_step(step):
        for piece in range(pieces):
            for way in range(2):
                if (way, step, piece) not in ring:
                    continue
                ring[way, step, piece].wait_recv()
                if step < groups // 2 - 2 or (step == groups // 2 - 2 and way == 2 * piece // pieces):
                    ring[way, step + 1, piece] = send_parent(way, step + 1, piece)

    for h in range(2):
        second_up[h].wait_recv()
        second_down[h].wait_recv()
    size = SIDE * part
    cut = size // 2
    rows_up, rows_down, rest_up, rest_down = [], [], [], []
    for h in range(2):
        at = row_start(h, outer_at[h])
        rows_up.append(pass_leaf(8 + h * 6, at, cut, near(h, 1, 0)))
        rows_down.append(pass_leaf(9 + h * 6, at + cut, size - cut, near(h, -1, 0)))
    for h in range(2):
        at = row_start(h, outer_at[h])
        rest_up.append(pass_leaf(10 + h * 6, at + cut, size - cut, near(h, 1, 0)))
        rest_down.append(pass_leaf(11 + h * 6, at, cut, near(h, -1, 0)))
    shared = [pass_leaf(20 + h * 4, row_start(h, outer_at[h]), size, sibling) for h in range(2)]

    row = lax.broadcasted_iota(jnp.int32, (rank, rank), 0)
    column = lax.broadcasted_iota(jnp.int32, (rank, rank), 1)
    low = rank // 2
    order = jnp.where(row < low, 2 * row, 2 * (row - low) + 1)
    shuffle = jnp.where(column == order, 1.0, 0.0).astype(BF16)

    @pl.loop(0, parent_count, unroll=6)
    def _(p):
        mixed = nn(shuffle, parent_change[p]).astype(BF16)
        for c in range(parent_links):
            parent_half_rows[p * parent_links + c] = nn(mixed, parent_blocks_ref[p, c]).astype(BF16)

    def leaf_halves(begin, end):
        @pl.loop(begin, end, unroll=3)
        def _(t):
            mixed = nn(shuffle, change[t]).astype(BF16)
            for c in range(links):
                half_rows[t * links + c] = nn(mixed, leaf_blocks_ref[t, c]).astype(BF16)

    ring_step(0)
    leaf_halves(0, 3)
    ring_step(1)
    leaf_halves(3, 6)
    ring_step(2)
    leaf_halves(6, 9)
    ring_step(3)
    leaf_halves(9, 12)
    last_up, last_down = [], []
    for h in range(2):
        rows_up[h].wait_recv()
        last_up.append(pass_leaf(12 + h * 6, row_start(h, outer_at[h] - 1), cut, near(h, 1, 0)))
        rows_down[h].wait_recv()
        last_down.append(
            pass_leaf(13 + h * 6, row_start(h, outer_at[h] + 1) + cut, size - cut, near(h, -1, 0))
        )
    ring_step(4)
    for h in range(2):
        rest_up[h].wait_recv()
        shared.append(pass_leaf(21 + h * 4, row_start(h, outer_at[h] - 1), size, sibling))
        rest_down[h].wait_recv()
        shared.append(pass_leaf(22 + h * 4, row_start(h, outer_at[h] + 1), size, sibling))
    ring_step(5)
    for h in range(2):
        last_up[h].wait_recv()
        last_down[h].wait_recv()
        shared.append(pass_leaf(23 + h * 4, row_start(h, outer_at[h] + 2), size, sibling))
    ring_step(6)
    for copy in shared:
        copy.wait_recv()
    for copy in loads[4:]:
        copy.wait()

    def couple(half_pair, distant):
        return nt(beside(half_pair[:low], half_pair[low:]), diagonal(distant, distant))

    def flatten(out, at, slot, width):
        for q in range(low):
            rows = staged[slot, pl.ds(q, width, stride=low), :]
            out[at, :, 2 * rank * q : 2 * rank * (q + 1)] = rows.astype(BF16)

    @pl.loop(0, count // 2)
    def _(pair):
        for slot in range(2):
            t = pair * 2 + slot
            for c in range(links):
                place, at = leaf_dev_ref[c, t], leaf_slot_ref[c, t]
                x, y, z = place // (2 * SIDE), place // 2 % SIDE, place % 2
                h = at // part
                outer, inner = y + h * (x - y), x + h * (y - x)
                index = (((h * 2 + z) * SIDE + outer) * SIDE + inner) * part + at - h * part
                staged[slot, low * c : low * (c + 1), :] = couple(half_rows[t * links + c], leaves[index])
        for slot in range(2):
            flatten(leaf_out, pair * 2 + slot, slot, links)

    ring_step(7)

    @pl.loop(0, parent_count // 2)
    def _(pair):
        for slot in range(2):
            p = pair * 2 + slot
            for c in range(parent_links):
                index = parent_group_ref[c, p] * parent_count + parent_slot_ref[c, p]
                staged[slot, low * c : low * (c + 1), :] = couple(
                    parent_half_rows[p * parent_links + c], parents[index]
                )
        for slot in range(2):
            flatten(parent_out, pair * 2 + slot, slot, parent_links)

    for copy in started:
        copy.wait_send()


def shards(
    leaf_bases,
    leaf_transfers,
    leaf_blocks,
    leaf_partner_dev,
    leaf_partner_slot,
    parent_blocks,
    parent_partner_group,
    parent_partner_slot,
    leaf_start,
    parent_start,
):
    leaf_count, leaf_links = leaf_blocks.shape[:2]
    half_count, parent_links = parent_blocks.shape[:2]
    rank_new, rank_old = leaf_start.shape
    points = leaf_bases.shape[1]
    groups, members = lax.axis_size("grp"), lax.axis_size("sub")
    square = (rank_old, rank_old)
    block = (rank_new, rank_old)
    paired = (rank_new, 2 * rank_new)

    def shape(*sizes):
        return pltpu.VMEM(sizes, BF16)

    def room(*sizes, dtype=BF16):
        return pltpu.VMEM(sizes, dtype)

    whole, outside = pl.BlockSpec(memory_space=pltpu.VMEM), pl.BlockSpec(memory_space=pl.ANY)
    indices = (leaf_partner_dev.T, leaf_partner_slot.T, parent_partner_group.T, parent_partner_slot.T)
    streams = (leaf_bases, leaf_transfers, leaf_blocks, parent_blocks)
    transfers = (2, 28, 3 * groups)
    return pl.pallas_call(
        functools.partial(kernel, groups),
        out_shape=(
            shape(leaf_count, rank_new, points),
            shape(leaf_count, leaf_links, rank_new * rank_new),
            shape(half_count, parent_links, rank_new * rank_new),
        ),
        in_specs=[outside] * 4 + [whole] * 2 + [outside] * 4,
        out_specs=(whole,) * 3,
        scratch_shapes=[pltpu.SMEM(values.shape, jnp.int32) for values in indices]
        + [room(*values.shape) for values in streams]
        + [
            room(members * leaf_count, *block),
            room(groups * half_count, *block),
            room(leaf_count, *block),
            room(half_count, *block),
            room(leaf_count * leaf_links, *block),
            room(half_count * parent_links, *block),
            room(2, leaf_links * rank_new // 2, 2 * rank_new, dtype=F32),
            room(half_count, *square),
            room(half_count, *square),
            room(half_count, *square),
            room(half_count, *block, dtype=F32),
            room(half_count, *block),
            room(half_count, *block),
            room(half_count, *square),
            room(half_count, *square),
            room(leaf_count, *block),
            room(leaf_count, *block),
            room(leaf_count // 2, *paired, dtype=F32),
            room(half_count, *block),
            room(half_count, *block),
            room(half_count // 2, *paired, dtype=F32),
            pltpu.SemaphoreType.DMA((8,)),
        ]
        + [pltpu.SemaphoreType.DMA((number,)) for number in transfers for _ in range(2)],
        compiler_params=pltpu.CompilerParams(collective_id=0, has_side_effects=True),
        name="recompress",
    )(*indices, leaf_start, parent_start, *streams)


def solution(mesh):
    placed = (
        P(("grp", "sub"), None, None),
        P(("grp", "sub"), None, None),
        P(("grp", "sub"), None, None, None),
        P(("grp", "sub"), None),
        P(("grp", "sub"), None),
        P(("grp", "sub"), None, None, None),
        P(("grp", "sub"), None),
        P(("grp", "sub"), None),
        P(),
        P(),
    )
    return jax.shard_map(
        shards,
        mesh=mesh,
        in_specs=placed,
        out_specs=(
            P(("grp", "sub"), None, None),
            P(("grp", "sub"), None, None),
            P(("grp", "sub"), None, None),
        ),
        check_vma=False,
    )
```
